32 devices in a mesh: subj: 4 (over y, x), vox: 8 (over z, core).
Axes of the slice: x: 2, y: 2, z: 4, core: 2. Of those that a mesh axis runs over, the one named last changes fastest.
Arguments:
- contrasts: bfloat16 [448, 16, 9919], P('subj', 'vox'), may hold values from -60 to 60
- flips: int32 [48, 448], P(None, 'subj'), may hold values from -1 to 1, as said below
- mask: int32 [16, 9919], P('vox'), may hold values 0 or 1
Outputs:
- highest: float32 [16, 9919], P('vox')
- exceed: float32 [16, 9919], P('vox')
The draws below stay inside these ranges and needn't reach their ends.
Inputs may be any that keep to these rules, and one draw needn't show every extreme that they name: `flips`: every entry is -1 or +1.
All inputs are finite; a program needn't handle non-finite values. No bound on the sum of `mask` on one device may be relied on, other than what follows from the above.
Results may differ from the reference program's by a relative error of at most 0.0003.
Values sent between devices are 32-bit elements; how exact they have to be, the bound alone decides.
No kernel may reach another device: no remote copies, remote signals or barrier semaphores. Data moves between devices by JAX's collectives and lax.ppermute only.
A program may use at most 64 MiB of HBM per device.

```python
import math
import jax
import jax.numpy as jnp
from jax import lax

S_DEV = 112
PY = 109
RADIUS = 2
FB = 16
NB = 3
NF = 48
PLANE = 9919
SUBJ = 448
NZ = 16
N_SUBJ = 4


def draw_contrasts(key, part):
    keys = jax.random.split(key, 4)
    voxel_scale = jnp.exp(jax.random.uniform(keys[0], (NZ, PLANE), jnp.float32, jnp.log(0.3), jnp.log(3.0)))
    subject_scale = jnp.exp(jax.random.uniform(keys[1], (SUBJ, 1, 1), jnp.float32, jnp.log(0.5), jnp.log(2.0)))
    spread_factor = 1.0 / SUBJ ** 0.5
    effect = jax.random.uniform(keys[2], (NZ, PLANE), jnp.float32, -3.0, 3.0) * spread_factor
    noise = jnp.clip(jax.random.normal(keys[3], (SUBJ, NZ, PLANE), jnp.float32), -5.0, 5.0)
    values = (effect[None] + noise * subject_scale) * voxel_scale[None]
    return values.astype(jnp.bfloat16)


def draw_flips(key, part):
    bits = jax.random.randint(jax.random.fold_in(key, 7), (NF, SUBJ), 0, 2, jnp.int32)
    return 2 * bits - 1


def touch_ends(values, key, least, high):
    place = [jax.random.randint(jax.random.fold_in(key, axis), (), 0, length) for axis, length in enumerate(values.shape)]
    main_axis = values.shape.index(max(values.shape))
    next_to = place[:main_axis] + [(place[main_axis] + 1) % values.shape[main_axis]] + place[main_axis + 1:]
    return values.at[tuple(place)].set(least).at[tuple(next_to)].set(high)


def setup_inputs(seed: int = 0) -> dict:
    seeds = jax.random.split(jax.random.key(seed), 4)
    return {
        "contrasts": draw_contrasts(jax.random.fold_in(seeds[3], 71), 0),
        "flips": draw_flips(jax.random.fold_in(seeds[3], 71), 0),
        "mask": touch_ends((jax.random.randint(seeds[2], (NZ, PLANE), 0, 4) < 3).astype(jnp.int32), jax.random.fold_in(seeds[2], 1), 0, 1),
    }


epsilon = 1e-06

def along_plane(volume, stride):
    margin = RADIUS * stride
    widths = [(0, 0)] * (volume.ndim - 1) + [(margin, margin)]
    padded = jnp.pad(volume, widths)
    length = volume.shape[-1]
    column = jnp.arange(length) % PY
    result = jnp.zeros(volume.shape, jnp.float32)
    for offset in range(-RADIUS, RADIUS + 1):
        begin = margin + offset * stride
        shifted = padded[..., begin:begin + length]
        if stride == 1:
            inside = (column + offset >= 0) & (column + offset < PY)
            shifted = jnp.where(inside, shifted, jnp.zeros_like(shifted))
        result = result + math.exp(-0.5 * offset * offset) * shifted
    return result

def along_depth(padded, depth):
    result = jnp.zeros((padded.shape[0], depth, padded.shape[2]), jnp.float32)
    for offset in range(-RADIUS, RADIUS + 1):
        result = result + math.exp(-0.5 * offset * offset) * padded[:, RADIUS + offset:RADIUS + offset + depth]
    return result

def depth_weights(positions, total):
    result = jnp.zeros(positions.shape, jnp.float32)
    for offset in range(-RADIUS, RADIUS + 1):
        inside = ((positions + offset >= 0) & (positions + offset < total)).astype(jnp.float32)
        result = result + math.exp(-0.5 * offset * offset) * inside
    return result

def smooth(volume):
    flat = along_plane(along_plane(volume, 1), PY)
    padded = jnp.pad(flat, ((0, 0), (RADIUS, RADIUS), (0, 0)))
    summed = along_depth(padded, NZ)
    plane_norm = along_plane(along_plane(jnp.ones((PLANE,), jnp.float32), 1), PY)
    depth_norm = depth_weights(jnp.arange(NZ, dtype=jnp.int32), NZ)
    return summed / (plane_norm[None, None, :] * depth_norm[None, :, None])

def reference(contrasts, flips, mask):
    values = contrasts.reshape(SUBJ, NZ * PLANE)
    totals = jnp.zeros((NF, NZ * PLANE), jnp.float32)
    linear = jnp.zeros((NZ * PLANE,), jnp.float32)
    second = jnp.zeros((NZ * PLANE,), jnp.float32)
    for block_index in range(N_SUBJ):
        block = values[block_index * S_DEV:(block_index + 1) * S_DEV].astype(jnp.float32)
        sign_rows = flips[:, block_index * S_DEV:(block_index + 1) * S_DEV].astype(jnp.float32)
        totals = totals + jnp.dot(sign_rows, block, precision=lax.Precision.HIGHEST)
        linear = linear + lax.optimization_barrier(jnp.sum(block, axis=0))
        second = second + lax.optimization_barrier(jnp.sum(block * block, axis=0))
    number = jnp.float32(SUBJ)
    second = second.reshape(1, NZ, PLANE)
    sigma = jnp.sqrt(smooth(second / number) + epsilon)[0]
    denominator = jnp.sqrt(number) * sigma
    observed = linear.reshape(NZ, PLANE) / denominator
    highest = jnp.full((NZ, PLANE), -1e+30, jnp.float32)
    exceed = jnp.zeros((NZ, PLANE), jnp.float32)
    for batch_index in range(NB):
        block_sums = totals[batch_index * FB:(batch_index + 1) * FB].reshape(FB, NZ, PLANE)
        tflip = block_sums / denominator[None]
        highest = jnp.maximum(highest, lax.optimization_barrier(jnp.max(tflip, axis=0)))
        exceed = exceed + lax.optimization_barrier(jnp.sum(jax.nn.sigmoid(2.0 * (tflip - observed[None])), axis=0))
    inside = mask.astype(jnp.float32)
    return (highest * inside, exceed / NF * inside)
```

```python
import functools
import math

import jax
import jax.numpy as jnp
from jax import lax
from jax.experimental import pallas as pl
from jax.experimental.pallas import tpu as pltpu
from jax.sharding import PartitionSpec as P

PY = 109
RADIUS = 2
FB = 16
NB = 3
NF = 48
BLOCK = 384
LANES = 128
VMEM_LIMIT = 24 * 1024 * 1024


epsilon = 1e-06


def weight(offset):
    return math.exp(-0.5 * offset * offset)


def padded_2(shard, sides, width):
    for axis, dim in sides:
        size, length = (lax.axis_size(axis), shard.shape[dim])
        up = [(i, (i + 1) % size) for i in range(size - 1)]
        down = [(j, i) for i, j in up]
        last = lax.slice_in_dim(shard, length - width, length, axis=dim)
        leading = lax.slice_in_dim(shard, 0, width, axis=dim)
        before = lax.ppermute(last, axis, up)
        after = lax.ppermute(leading, axis, down)
        shard = jnp.concatenate([before, shard, after], axis=dim)
    return shard


def along_plane(volume, stride):
    margin = RADIUS * stride
    widths = [(0, 0)] * (volume.ndim - 1) + [(margin, margin)]
    padded = jnp.pad(volume, widths)
    length = volume.shape[-1]
    column = jnp.arange(length) % PY
    result = jnp.zeros(volume.shape, jnp.float32)
    for offset in range(-RADIUS, RADIUS + 1):
        begin = margin + offset * stride
        shifted = padded[..., begin : begin + length]
        if stride == 1:
            inside = (column + offset >= 0) & (column + offset < PY)
            shifted = jnp.where(inside, shifted, jnp.zeros_like(shifted))
        result = result + weight(offset) * shifted
    return result


def depth_weights(positions, total):
    result = jnp.zeros(positions.shape, jnp.float32)
    for offset in range(-RADIUS, RADIUS + 1):
        inside = ((positions + offset >= 0) & (positions + offset < total)).astype(jnp.float32)
        result = result + weight(offset) * inside
    return result


def smooth(volume, norm_all):
    flat = along_plane(along_plane(volume, 1), PY)
    padded = padded_2(flat, (("vox", 1),), RADIUS)
    depth = volume.shape[1]
    summed = jnp.zeros(volume.shape, jnp.float32)
    for offset in range(-RADIUS, RADIUS + 1):
        summed = summed + weight(offset) * padded[:, RADIUS + offset : RADIUS + offset + depth]
    return summed / norm_all


def per_device_any(contrasts, flips, mask):
    local_subjects, depth, plane_cells = contrasts.shape
    groups = lax.axis_size("subj")
    number = jnp.float32(local_subjects * groups)
    values = contrasts.reshape(local_subjects, depth * plane_cells)
    unity = jnp.ones((1, local_subjects), jnp.bfloat16)
    linear = jnp.dot(unity, values, preferred_element_type=jnp.float32)[0]
    squared = jnp.sum(jnp.square(values.astype(jnp.float32)), axis=0)
    linear, second = lax.psum((linear, squared), "subj")
    positions = lax.axis_index("vox") * depth + jnp.arange(depth, dtype=jnp.int32)
    depth_norm = depth_weights(positions, depth * lax.axis_size("vox"))
    plane_norm = along_plane(along_plane(jnp.ones((plane_cells,), jnp.float32), 1), PY)
    norm_all = plane_norm[None, None, :] * depth_norm[None, :, None]
    second = second.reshape(1, depth, plane_cells)
    sigma = jnp.sqrt(smooth(second / number, norm_all) + epsilon)[0]
    denominator = jnp.sqrt(number) * sigma
    observed = linear.reshape(depth, plane_cells) / denominator
    highest = jnp.full((depth, plane_cells), -1e30, jnp.float32)
    exceed = jnp.zeros((depth, plane_cells), jnp.float32)
    for batch_index in range(NB):
        sign_rows = flips[batch_index * FB : (batch_index + 1) * FB].astype(jnp.bfloat16)
        partial_value = jnp.dot(sign_rows, values, preferred_element_type=jnp.float32)
        block_sums = lax.psum(partial_value, "subj")
        tflip = block_sums.reshape(-1, depth, plane_cells) / denominator[None]
        highest = jnp.maximum(highest, jnp.max(tflip, axis=0))
        exceed = exceed + jnp.sum(jax.nn.sigmoid(2.0 * (tflip - observed[None])), axis=0)
    inside = mask.astype(jnp.float32)
    return (highest * inside, exceed / NF * inside)


def params():
    return pltpu.CompilerParams(vmem_limit_bytes=VMEM_LIMIT)


def chunk_kernel(colour, where, flips_ref, lower_ref, upper_ref, send_ref, keep_ref, extra_ref):
    subjects = flips_ref.shape[1]
    signs = flips_ref[...].astype(jnp.bfloat16)
    subject = lax.broadcasted_iota(jnp.int32, (subjects, 2 * subjects), 0)
    row = lax.broadcasted_iota(jnp.int32, (subjects, 2 * subjects), 1)

    def spread(plane):
        pick = (row == 2 * subject + plane).astype(jnp.bfloat16)
        return jnp.dot(signs, pick, preferred_element_type=jnp.float32).astype(jnp.bfloat16)

    half = where[1]
    plane = where[0]
    parity = lax.broadcasted_iota(jnp.int32, (8, 2 * subjects), 1) % 2
    both = (parity == lax.broadcasted_iota(jnp.int32, (8, 2 * subjects), 0)).astype(jnp.bfloat16)
    if colour == 0:
        rows = jnp.concatenate([spread(1 - plane), spread(plane), both], axis=0)
    else:
        rows = jnp.concatenate([spread(0), spread(1), both], axis=0)
    count = signs.shape[0]
    for side, ref in enumerate((lower_ref, upper_ref)):
        block = ref[...].reshape(2 * subjects, ref.shape[2])
        sums = jnp.dot(rows, block, preferred_element_type=jnp.float32)
        if colour == 0:
            send_ref[side] = sums[:count]
            keep_ref[side] = sums[count : 2 * count]
        else:
            target = send_ref if side == 0 else keep_ref
            target[0] = sums[:count]
            target[1] = sums[count : 2 * count]
        wide = block.astype(jnp.float32)
        square = jnp.sum((wide * wide).reshape(-1, 8, wide.shape[1]), axis=0)
        square = square[0:4] + square[4:8]
        square = square[0:2] + square[2:4]
        place = side if colour == 0 else (1 - half if side == 0 else half)
        extra_ref[place, 0:2] = sums[2 * count : 2 * count + 2]
        extra_ref[place, 2:4] = square


def chunk(colour, first, steps, blocks, where, flips, contrasts):
    subjects = contrasts.shape[0]
    flip_count = flips.shape[0]
    width = steps * BLOCK

    def lower(i, w):
        return (0, 0, first + i + (0 if colour == 0 else blocks * (1 - w[1])))

    def upper(i, w):
        return (0, 0, first + i + (blocks if colour == 0 else blocks * w[1]))

    out = jax.ShapeDtypeStruct((2, flip_count, width), jnp.float32)
    out_spec = pl.BlockSpec((2, flip_count, BLOCK), lambda i, w: (0, 0, i))
    return pl.pallas_call(
        functools.partial(chunk_kernel, colour),
        grid_spec=pltpu.PrefetchScalarGridSpec(
            num_scalar_prefetch=1,
            grid=(steps,),
            in_specs=[
                pl.BlockSpec((flip_count, subjects), lambda i, w: (0, 0)),
                pl.BlockSpec((subjects, 2, BLOCK), lower),
                pl.BlockSpec((subjects, 2, BLOCK), upper),
            ],
            out_specs=[
                out_spec,
                out_spec,
                pl.BlockSpec((2, 4, BLOCK), lambda i, w: (0, 0, i)),
            ],
        ),
        out_shape=[out, out, jax.ShapeDtypeStruct((2, 4, width), jnp.float32)],
        compiler_params=params(),
        name=f"chunk{colour}_{first}",
    )(where, flips, contrasts, contrasts)


def plane_kernel(cells, count, *refs):
    extras, (flat_ref,) = refs[:count], refs[count:]
    length = sum(r.shape[2] for r in extras)
    total = flat_ref.shape[1]
    pieces = [r[side, 2:4] for side in (0, 1) for r in extras]
    pieces.append(jnp.zeros((2, total - 2 * length), jnp.float32))
    planes = jnp.concatenate(pieces, axis=1)
    planes = jnp.concatenate([planes, jnp.ones((6, total), jnp.float32)], axis=0)
    index = lax.broadcasted_iota(jnp.int32, (8, total), 1)
    planes = jnp.where(index < cells, planes, 0.0)
    column = index % PY
    result = planes
    for offset in (-2, -1, 1, 2):
        moved = pltpu.roll(planes, (-offset) % total, 1)
        inside = (column + offset >= 0) & (column + offset < PY)
        result = result + weight(offset) * jnp.where(inside, moved, 0.0)
    planes = jnp.where(index < cells, result, 0.0)
    result = planes
    for offset in (-2, -1, 1, 2):
        result = result + weight(offset) * pltpu.roll(planes, (-offset * PY) % total, 1)
    flat_ref[...] = result


def depth_kernel(count, where, flat_ref, before_ref, after_ref, *refs):
    extras, (send_ref, keep_ref) = refs[:count], refs[count:]
    length = send_ref.shape[1]
    before = [before_ref[i : i + 1, :length] for i in range(2)]
    own = [flat_ref[i : i + 1, :length] for i in range(2)]
    after = [after_ref[i : i + 1, :length] for i in range(2)]
    stack = before + own + after
    sums = []
    for plane in range(2):
        total = jnp.zeros_like(own[0])
        for offset in range(-RADIUS, RADIUS + 1):
            total = total + weight(offset) * stack[RADIUS + plane + offset]
        sums.append(total)
    linear = [
        jnp.concatenate([r[side, i : i + 1] for side in (0, 1) for r in extras], axis=1)
        for i in range(2)
    ]
    plane = where[0]

    @pl.when(plane == 0)
    def _():
        for ref, i in ((keep_ref, 0), (send_ref, 1)):
            ref[0:1] = linear[i]
            ref[1:2] = sums[i]

    @pl.when(plane == 1)
    def _():
        for ref, i in ((keep_ref, 1), (send_ref, 0)):
            ref[0:1] = linear[i]
            ref[1:2] = sums[i]


def half_kernel(where, keep_ref, got_ref, flat_ref, send_ref, mine_ref):
    length = send_ref.shape[1]
    half = where[1]
    total = keep_ref[...] + got_ref[...]

    @pl.when(half == 0)
    def _():
        send_ref[...] = total[:, length:]
        mine_ref[0:2] = total[:, :length]
        mine_ref[2:3] = flat_ref[2:3, :length]

    @pl.when(half == 1)
    def _():
        send_ref[...] = total[:, :length]
        mine_ref[0:2] = total[:, length:]
        mine_ref[2:3] = flat_ref[2:3, length : 2 * length]


def final_kernel(subjects, planes, where, keep_ref, got_ref, last_ref, mine_ref, other_ref, out_ref):
    totals = keep_ref[...] + got_ref[...] + last_ref[...]
    linear = mine_ref[0:1] + other_ref[0:1]
    smoothed = mine_ref[1:2] + other_ref[1:2]
    position = where[2] * 2 + where[0]
    depth_norm = jnp.float32(0.0)
    for offset in range(-RADIUS, RADIUS + 1):
        inside = (position + offset >= 0) & (position + offset < planes)
        depth_norm = depth_norm + jnp.where(inside, jnp.float32(weight(offset)), jnp.float32(0.0))
    norm = mine_ref[2:3] * depth_norm
    sigma = jnp.sqrt(smoothed / subjects / norm + epsilon)
    inverse = 1.0 / (math.sqrt(subjects) * sigma)
    scaled = totals * inverse
    observed = linear * inverse
    out_ref[0:1] = jnp.max(scaled, axis=0, keepdims=True)
    share = 1.0 / (1.0 + jnp.exp(-2.0 * (scaled - observed)))
    out_ref[1:2] = jnp.sum(share, axis=0, keepdims=True) / totals.shape[0]


def final(colour, first, steps, subjects, planes, where, keep, got, last, mine, other):
    flip_count = keep.shape[1]
    width = steps * BLOCK

    def pick(i, w):
        return (w[1] if colour == 0 else w[0], 0, i)

    chosen = pl.BlockSpec((None, flip_count, BLOCK), pick)
    return pl.pallas_call(
        functools.partial(final_kernel, subjects, planes),
        grid_spec=pltpu.PrefetchScalarGridSpec(
            num_scalar_prefetch=1,
            grid=(steps,),
            in_specs=[
                chosen,
                chosen,
                pl.BlockSpec((flip_count, BLOCK), lambda i, w: (0, i)),
                pl.BlockSpec((3, BLOCK), lambda i, w: (0, first + i)),
                pl.BlockSpec((2, BLOCK), lambda i, w: (0, first + i)),
            ],
            out_specs=pl.BlockSpec((2, BLOCK), lambda i, w: (0, i)),
        ),
        out_shape=jax.ShapeDtypeStruct((2, width), jnp.float32),
        compiler_params=params(),
        name=f"final{colour}_{first}",
    )(where, keep, got, last, mine, other)


def merge_kernel(where, mask_ref, own_ref, across_ref, along_ref, far_ref, high_ref, share_ref):
    length = own_ref.shape[1]
    cells = high_ref.shape[1]
    plane, half = where[0], where[1]
    blocks = {(0, 0): own_ref, (1, 0): across_ref, (0, 1): along_ref, (1, 1): far_ref}
    inside = mask_ref[...].astype(jnp.float32)
    for is_plane in range(2):
        for is_half in range(2):

            @pl.when((plane == is_plane) & (half == is_half))
            def _(is_plane=is_plane, is_half=is_half):
                rows = [[], []]
                for p in range(2):
                    parts = [blocks[(p ^ is_plane, h ^ is_half)][...] for h in range(2)]
                    whole = jnp.concatenate(parts, axis=1)[:, :cells]
                    for out in range(2):
                        rows[out].append(whole[out : out + 1])
                high_ref[...] = jnp.concatenate(rows[0], axis=0) * inside
                share_ref[...] = jnp.concatenate(rows[1], axis=0) * inside


def small(kernel, where, operands, outs, name):
    return pl.pallas_call(
        kernel,
        grid_spec=pltpu.PrefetchScalarGridSpec(
            num_scalar_prefetch=1,
            grid=(1,),
            in_specs=[pl.BlockSpec(o.shape, lambda i, w, n=o.ndim: (0,) * n) for o in operands],
            out_specs=[pl.BlockSpec(s, lambda i, w, n=len(s): (0,) * n) for s in outs],
        ),
        out_shape=[jax.ShapeDtypeStruct(s, jnp.float32) for s in outs],
        compiler_params=params(),
        name=name,
    )(where, *operands)


def per_device_four(contrasts, flips, mask):
    local_subjects, depth, cells = contrasts.shape
    subjects = local_subjects * 4
    place = lax.axis_index("subj")
    plane, half = place % 2, place // 2
    vox, vox_size = lax.axis_index("vox"), lax.axis_size("vox")
    planes = depth * vox_size
    where = jnp.stack([plane, half, vox]).astype(jnp.int32)
    swap = [[(i, i ^ bit) for i in range(4)] for bit in (1, 2, 3)]
    blocks = pl.cdiv(cells, 2 * BLOCK)
    length = blocks * BLOCK
    parts = 4
    cuts = [blocks * i // parts for i in range(parts + 1)]
    chunks = [(i % 2, cuts[i], cuts[i + 1] - cuts[i]) for i in range(parts)]

    made = [chunk(c, f, n, blocks, where, flips, contrasts) for c, f, n in chunks]
    got = [lax.ppermute(m[0], "subj", swap[c]) for m, (c, f, n) in zip(made, chunks)]
    seconds = []
    for m, g, (colour, f, n) in zip(made, got, chunks):
        other = 1 - (half if colour == 0 else plane)
        send = lax.dynamic_index_in_dim(m[1], other, 0, False) + lax.dynamic_index_in_dim(g, other, 0, False)
        seconds.append(lax.ppermute(send, "subj", swap[1 - colour]))

    extras = [m[2] for m in made]
    total = pl.cdiv(cells + RADIUS * PY, LANES) * LANES
    total = max(total, 2 * length)
    if total - cells < RADIUS * PY:
        total += LANES * 2
    (flat,) = pl.pallas_call(
        functools.partial(plane_kernel, cells, len(extras)),
        out_shape=[jax.ShapeDtypeStruct((8, total), jnp.float32)],
        compiler_params=params(),
        name="plane",
    )(*extras)
    two = flat[0:2, : 2 * length]
    up = [(i, i + 1) for i in range(vox_size - 1)]
    down = [(i + 1, i) for i in range(vox_size - 1)]
    before = lax.ppermute(two, "vox", up)
    after = lax.ppermute(two, "vox", down)
    send, keep = small(
        functools.partial(depth_kernel, len(extras)),
        where,
        [flat, before, after, *extras],
        [(2, 2 * length), (2, 2 * length)],
        "depth",
    )
    arrived = lax.ppermute(send, "subj", swap[0])
    send, mine = small(half_kernel, where, [keep, arrived, flat], [(2, length), (3, length)], "half")
    other = lax.ppermute(send, "subj", swap[1])

    outs = [
        final(c, f, n, subjects, planes, where, m[1], g, s, mine, other)
        for m, g, s, (c, f, n) in zip(made, got, seconds, chunks)
    ]
    own = jnp.concatenate(outs, axis=1)
    across, along, far = (lax.ppermute(own, "subj", s) for s in swap)
    return tuple(
        small(merge_kernel, where, [mask, own, across, along, far], [mask.shape, mask.shape], "merge")
    )


def solution(mesh):
    in_specs = (P("subj", "vox", None), P(None, "subj"), P("vox", None))
    out_specs = (P("vox", None), P("vox", None))

    def per_device(contrasts, flips, mask):
        if lax.axis_size("subj") == 4 and contrasts.shape[1] == RADIUS == 2:
            return per_device_four(contrasts, flips, mask)
        return per_device_any(contrasts, flips, mask)

    return jax.shard_map(
        per_device, mesh=mesh, in_specs=in_specs, out_specs=out_specs, check_vma=False
    )
```
